768 devices in a mesh: seg: 96 (over z, y_lo, core), sub: 8 (over x, y_hi).
Axes of the slice: x: 4, y: 8 (y_hi: 2, y_lo: 4; y = y_hi * 4 + y_lo), z: 12, core: 2. Of those that a mesh axis runs over, the one named last changes fastest.
Arguments:
- state: bfloat16 [4, 128, 1572864], P(None, None, ('seg', 'sub')), may hold values from -6 to 6
- sun_frac: bfloat16 [1572864], P(('seg', 'sub')), may hold values from 0.049804688 to 0.94921875
- land_count: int32 [768], replicated, may hold values from 0 to 2048, as said below
- mixing: bfloat16 [512, 512], replicated, may hold values from -0.25 to 0.25
- canopy_sun: bfloat16 [128, 128], replicated, may hold values from -0.5 to 0.5
- canopy_shade: bfloat16 [128, 128], replicated, may hold values from -0.5 to 0.5
- bias_sun: float32 [128], replicated, may hold values from -3 to 3
- bias_shade: float32 [128], replicated, may hold values from -3 to 3
Outputs:
- tendency: bfloat16 [4, 128, 1572864], P(None, None, ('seg', 'sub'))
The draws below stay inside these ranges and needn't reach their ends.
Inputs may be any that keep to these rules, and one draw needn't show every extreme that they name: `land_count`: land columns come first in each group.
All inputs are finite; a program needn't handle non-finite values.
Results may differ from the reference program's by a relative error of at most 0.0035.
Values may be sent and summed in bfloat16 or wider, within the bound.
No kernel may reach another device: no remote copies, remote signals or barrier semaphores. Data moves between devices by JAX's collectives and lax.ppermute only.
A program may use at most 32 MiB of HBM per device.

```python
import jax
import jax.numpy as jnp
from jax import lax

FIELDS = 4
LEV = 128
CANLEV = 32
ITERS = 4
EDGE = 128
COLS_DEV = 2048
GROUPS = 768
COLUMNS = 1572864
N_SEG = 96
N_SUB = 8


def draw_land_count(key, part):
    stretch = 16
    coarse_count = GROUPS // stretch + 2
    first_key = jax.random.fold_in(key, 11)
    second_key = jax.random.fold_in(key, 23)
    levels = jax.random.randint(first_key, (coarse_count,), 0, COLS_DEV + 1)
    position = jnp.arange(GROUPS, dtype=jnp.int32)
    coarse_index = position // stretch
    within = position % stretch
    lower_level = levels[coarse_index]
    upper_level = levels[coarse_index + 1]
    smooth = (lower_level * (stretch - within) + upper_level * within) // stretch
    jitter = jax.random.randint(second_key, (GROUPS,), -(COLS_DEV // 8), COLS_DEV // 8 + 1)
    counts = jnp.clip(smooth + jitter, 0, COLS_DEV).astype(jnp.int32)
    segments = GROUPS // N_SUB
    last_group = GROUPS - 1
    last_far = (segments // 2 - 1) * N_SUB + N_SUB - 1
    last_near = (segments - 1) * N_SUB + N_SUB // 2 - 1
    first_far = segments // 2 * N_SUB
    first_near = N_SUB // 2
    counts = counts.at[last_far].set(0).at[last_near].set(0)
    counts = counts.at[first_far].set(0).at[first_near].set(0)
    counts = counts.at[last_group].set(COLS_DEV).at[0].set(COLS_DEV)
    return counts.astype(jnp.int32)


def shard_levels(stream_key, extent, split, low, largest):
    def one(dim, blocks):
        draws = jax.random.uniform(jax.random.fold_in(jax.random.fold_in(stream_key, 6), dim), (blocks,), jnp.float32, low / len(split), largest / len(split))
        return jnp.repeat(jnp.exp(draws), extent[dim] // blocks).reshape((-1,) + (1,) * (len(extent) - dim - 1))

    factor_of = one(*split[0])
    for cut in split[1:]:
        factor_of = factor_of * one(*cut)
    return factor_of


def scatter_about(stream_key, dims, deviation, bound, shards=(), kind=jnp.bfloat16):
    values = deviation * jax.random.normal(stream_key, dims, jnp.float32)
    if shards:
        values = values * shard_levels(stream_key, dims, shards, -0.22, 0.18)
    return jnp.clip(values, -bound, bound).astype(kind)


def setup_inputs(seed: int = 0) -> dict:
    arg_keys = jax.random.split(jax.random.key(seed), 9)
    return {
        "state": scatter_about(arg_keys[0], (FIELDS, LEV, COLUMNS), 1.0, 6.0, ((2, 768),)),
        "sun_frac": jnp.clip(0.049804688 + 0.89941406 * jax.random.uniform(arg_keys[1], (COLUMNS,), jnp.float32) ** shard_levels(arg_keys[1], (COLUMNS,), ((0, 768),), -0.2, 0.2), 0.049804688, 0.94921875).astype(jnp.bfloat16),
        "land_count": draw_land_count(jax.random.fold_in(arg_keys[8], 71), 0),
        "mixing": scatter_about(arg_keys[3], (FIELDS * LEV, FIELDS * LEV), (FIELDS * LEV) ** -0.5, 0.25),
        "canopy_sun": scatter_about(arg_keys[4], (FIELDS * CANLEV, FIELDS * CANLEV), (FIELDS * CANLEV) ** -0.5, 0.5),
        "canopy_shade": scatter_about(arg_keys[5], (FIELDS * CANLEV, FIELDS * CANLEV), (FIELDS * CANLEV) ** -0.5, 0.5),
        "bias_sun": scatter_about(arg_keys[6], (FIELDS * CANLEV,), 0.5, 3.0, (), jnp.float32),
        "bias_shade": scatter_about(arg_keys[7], (FIELDS * CANLEV,), 0.5, 3.0, (), jnp.float32),
    }


def canopy(low, frac, land, canopy_sun, canopy_shade, bias_sun, bias_shade):
    current = low
    for step in range(ITERS):
        rounded = current.astype(jnp.bfloat16)
        sunny = jnp.tanh(jnp.dot(canopy_sun, rounded, preferred_element_type=jnp.float32) + bias_sun[:, None])
        shady = jnp.tanh(jnp.dot(canopy_shade, rounded, preferred_element_type=jnp.float32) + bias_shade[:, None])
        current = current + 0.5 * (frac * sunny + (1.0 - frac) * shady)
    return jnp.where(land, current - low, jnp.zeros_like(low)).astype(jnp.bfloat16)


def physics(cols, frac_b, land, mixing, canopy_sun, canopy_shade, bias_sun, bias_shade):
    count = cols.shape[2]
    raw = jnp.dot(mixing, cols.reshape(FIELDS * LEV, count), preferred_element_type=jnp.float32)
    raw = raw.reshape(FIELDS, LEV, count)
    low = cols[:, LEV - CANLEV:, :].reshape(FIELDS * CANLEV, count).astype(jnp.float32)
    frac = frac_b.astype(jnp.float32)
    added = canopy(low, frac, land, canopy_sun, canopy_shade, bias_sun, bias_shade)
    added = added.astype(jnp.float32).reshape(FIELDS, CANLEV, count)
    return raw.at[:, LEV - CANLEV:, :].add(added)


def reference(state, sun_frac, land_count, mixing, canopy_sun, canopy_shade, bias_sun, bias_shade):
    groups = N_SEG * N_SUB
    blocks = state.reshape(FIELDS, LEV, groups, COLS_DEV).transpose(2, 0, 1, 3)
    fracs = sun_frac.reshape(groups, COLS_DEV)
    column = jnp.arange(COLS_DEV, dtype=jnp.int32)
    params = (mixing, canopy_sun, canopy_shade, bias_sun, bias_shade)

    def rims(items):
        block, frac, count = items
        land = column < count
        first = physics(block[:, :, :EDGE], frac[:EDGE], land[:EDGE], *params)
        last = physics(block[:, :, COLS_DEV - EDGE:], frac[COLS_DEV - EDGE:], land[COLS_DEV - EDGE:], *params)
        return first, last

    firsts, lasts = lax.map(rims, (blocks, fracs, land_count))
    before = jnp.roll(lasts, 1, axis=0)
    after = jnp.roll(firsts, -1, axis=0)

    def whole(items):
        block, frac, count, left, right = items
        land = column < count
        raw = physics(block, frac, land, *params)
        raw = raw.at[:, :, :EDGE].add(left)
        raw = raw.at[:, :, COLS_DEV - EDGE:].add(right)
        return raw.astype(jnp.bfloat16)

    result = lax.map(whole, (blocks, fracs, land_count, before, after))
    return result.transpose(1, 2, 0, 3).reshape(FIELDS, LEV, groups * COLS_DEV)
```

```python
import jax
import jax.numpy as jnp
from jax import lax
from jax.experimental import pallas as pl
from jax.experimental.pallas import tpu as pltpu
from jax.sharding import PartitionSpec as P

FIELDS = 4
LEV = 128
CANLEV = 32
ITERS = 4
EDGE = 128
ROWS = FIELDS * LEV
BLOCK = 256
AXES = ("seg", "sub")


def canopy_rows(values):
    return jnp.concatenate(
        [values[f * LEV + LEV - CANLEV : (f + 1) * LEV] for f in range(FIELDS)], axis=0
    )


def physics(cols, frac, land, mixing, pair, bias):
    raw = jnp.dot(mixing, cols, preferred_element_type=jnp.float32)
    rounded = canopy_rows(cols)
    low = rounded.astype(jnp.float32)
    half = low.shape[0]
    of_sun = 0.5 * frac
    of_shade = 0.5 - of_sun
    current = low
    for step in range(ITERS):
        if step:
            rounded = current.astype(jnp.bfloat16)
        drive = jnp.tanh(jnp.dot(pair, rounded, preferred_element_type=jnp.float32) + bias)
        current = current + (of_sun * drive[:half] + of_shade * drive[half:])
    added = jnp.where(land, current - low, 0.0).astype(jnp.bfloat16).astype(jnp.float32)
    parts = []
    for f in range(FIELDS):
        top = f * LEV + LEV - CANLEV
        parts.append(raw[f * LEV : top])
        parts.append(raw[top : (f + 1) * LEV] + added[f * CANLEV : (f + 1) * CANLEV])
    return jnp.concatenate(parts, axis=0)


def parameters(mixing_ref, sun_ref, shade_ref, bias_sun_ref, bias_shade_ref, count):
    pair = jnp.concatenate([sun_ref[...], shade_ref[...]], axis=0)
    rows = sun_ref.shape[0]
    bias = jnp.concatenate(
        [
            jnp.broadcast_to(bias_sun_ref[...], (rows, rows)).T,
            jnp.broadcast_to(bias_shade_ref[...], (rows, rows)).T,
        ],
        axis=0,
    )
    return mixing_ref[...], pair, jnp.concatenate([bias] * (count // rows), axis=1)


def group_here(offset):
    nsub = lax.axis_size("sub")
    groups = nsub * lax.axis_size("seg")
    return (lax.axis_index("seg") * nsub + lax.axis_index("sub") + groups + offset) % groups


def own_kernel(land_ref, cols_ref, frac_ref, mixing_ref, sun_ref, shade_ref, bs_ref, bh_ref, out_ref, first_ref, last_ref):
    step = pl.program_id(0)
    width = cols_ref.shape[1]
    params = parameters(mixing_ref, sun_ref, shade_ref, bs_ref, bh_ref, width)
    count = land_ref[group_here(0)]
    land = step * width + lax.broadcasted_iota(jnp.int32, (1, width), 1) < count
    raw = physics(cols_ref[...], frac_ref[...].astype(jnp.float32), land, *params)
    out_ref[...] = raw.astype(jnp.bfloat16)

    @pl.when(step == 0)
    def _():
        first_ref[...] = raw[:, :EDGE]

    @pl.when(step == pl.num_programs(0) - 1)
    def _():
        last_ref[...] = raw[:, width - EDGE :]


def edge_kernel(offset, start, land_ref, got_ref, own_ref, mixing_ref, sun_ref, shade_ref, bs_ref, bh_ref, all_ref, out_ref):
    del all_ref
    params = parameters(mixing_ref, sun_ref, shade_ref, bs_ref, bh_ref, EDGE)
    count = land_ref[group_here(offset)]
    land = start + lax.broadcasted_iota(jnp.int32, (1, EDGE), 1) < count
    frac = got_ref[ROWS : ROWS + 1, :].astype(jnp.float32)
    raw = physics(got_ref[:ROWS, :], frac, land, *params)
    out_ref[...] = (own_ref[...] + raw).astype(jnp.bfloat16)


def whole(shape):
    return pl.BlockSpec(shape, lambda *_: (0,) * len(shape))


def per_device(state, sun_frac, land_count, mixing, canopy_sun, canopy_shade, bias_sun, bias_shade):
    width = state.shape[2]
    half = FIELDS * CANLEV
    cols = state.reshape(ROWS, width)
    groups = lax.axis_size(AXES)
    up = [(i, (i + 1) % groups) for i in range(groups)]
    down = [(b, a) for a, b in up]

    def packed(start):
        edge = lax.slice_in_dim(cols, start, start + EDGE, axis=1)
        share = lax.slice_in_dim(sun_frac, start, start + EDGE, axis=0)
        return jnp.concatenate([edge, jnp.broadcast_to(share[None, :], (16, EDGE))], axis=0)

    from_left = lax.ppermute(packed(width - EDGE), AXES, up)
    from_right = lax.ppermute(packed(0), AXES, down)
    params = (mixing, canopy_sun, canopy_shade, bias_sun.reshape(1, half), bias_shade.reshape(1, half))
    param_specs = [whole((ROWS, ROWS)), whole((half, half)), whole((half, half)), whole((1, half)), whole((1, half))]
    steps = width // BLOCK
    out, first, last = pl.pallas_call(
        own_kernel,
        out_shape=(
            jax.ShapeDtypeStruct((ROWS, width), jnp.bfloat16),
            jax.ShapeDtypeStruct((ROWS, EDGE), jnp.float32),
            jax.ShapeDtypeStruct((ROWS, EDGE), jnp.float32),
        ),
        grid_spec=pltpu.PrefetchScalarGridSpec(
            num_scalar_prefetch=1,
            grid=(steps,),
            in_specs=[
                pl.BlockSpec((ROWS, BLOCK), lambda i, *_: (0, i)),
                pl.BlockSpec((1, BLOCK), lambda i, *_: (0, i)),
                *param_specs,
            ],
            out_specs=[
                pl.BlockSpec((ROWS, BLOCK), lambda i, *_: (0, i)),
                whole((ROWS, EDGE)),
                whole((ROWS, EDGE)),
            ],
        ),
        compiler_params=pltpu.CompilerParams(dimension_semantics=("arbitrary",)),
        name="own_columns",
    )(land_count, cols, sun_frac.reshape(1, width), *params)

    def with_edge(out, got, own, offset, start, block, name):
        def body(*refs):
            edge_kernel(offset, start, *refs)

        return pl.pallas_call(
            body,
            out_shape=jax.ShapeDtypeStruct((ROWS, width), jnp.bfloat16),
            grid_spec=pltpu.PrefetchScalarGridSpec(
                num_scalar_prefetch=1,
                grid=(1,),
                in_specs=[
                    whole(got.shape),
                    whole((ROWS, EDGE)),
                    *param_specs,
                    pl.BlockSpec(memory_space=pl.ANY),
                ],
                out_specs=pl.BlockSpec((ROWS, EDGE), lambda i, *_: (0, block)),
            ),
            input_output_aliases={8: 0},
            compiler_params=pltpu.CompilerParams(dimension_semantics=("arbitrary",)),
            name=name,
        )(land_count, got, own, *params, out)

    out = with_edge(out, from_left, first, -1, width - EDGE, 0, "left_edge")
    out = with_edge(out, from_right, last, 1, 0, width // EDGE - 1, "right_edge")
    return out.reshape(state.shape)


def solution(mesh):
    in_specs = (P(None, None, AXES), P(AXES), P(), P(), P(), P(), P(), P())
    out_specs = P(None, None, AXES)
    return jax.shard_map(
        per_device, mesh=mesh, in_specs=in_specs, out_specs=out_specs, check_vma=False
    )
```

```python
import jax
import jax.numpy as jnp
from jax import lax
from jax.experimental import pallas as pl
from jax.experimental.pallas import tpu as pltpu
from jax.sharding import PartitionSpec as P

FIELDS = 4
LEV = 128
CANLEV = 32
ITERS = 4
EDGE = 128
ROWS = FIELDS * LEV
HALF = FIELDS * CANLEV
CHUNK = 256
VMEM_BYTES = 16 * 2**20
AXES = ("seg", "sub")
F32 = jnp.float32
BF16 = jnp.bfloat16


def canopy_rows(values):
    return jnp.concatenate(
        [values[f * LEV + LEV - CANLEV : (f + 1) * LEV] for f in range(FIELDS)], axis=0
    )


def physics(cols, frac, land, mixing, pair, bias):
    raw = jnp.dot(mixing, cols, preferred_element_type=F32)
    rounded = canopy_rows(cols)
    low = rounded.astype(F32)
    of_sun = 0.5 * frac
    of_shade = 0.5 - of_sun
    current = low
    for step in range(ITERS):
        if step:
            rounded = current.astype(BF16)
        drive = jnp.tanh(jnp.dot(pair, rounded, preferred_element_type=F32) + bias)
        current = current + (of_sun * drive[:HALF] + of_shade * drive[HALF:])
    added = jnp.where(land, current - low, 0.0).astype(BF16).astype(F32)
    parts = []
    for f in range(FIELDS):
        top = f * LEV + LEV - CANLEV
        parts.append(raw[f * LEV : top])
        parts.append(raw[top : (f + 1) * LEV] + added[f * CANLEV : (f + 1) * CANLEV])
    return jnp.concatenate(parts, axis=0)


def group_here():
    return lax.axis_index("seg") * lax.axis_size("sub") + lax.axis_index("sub")


def lanes():
    return lax.broadcasted_iota(jnp.int32, (1, EDGE), 1)


def edges_kernel(
    land_ref, cols_ref, frac_ref, mixing_ref, sun_ref, shade_ref, bias_sun_ref, bias_shade_ref,
    send_first, send_last, raw_first, raw_last, mixing_out, pair_out, bias_out, frac_out, land_out, inner_out,
    cols_buf, frac_buf, bias_buf, land_buf, sems,
):
    width = cols_ref.shape[1]
    moves = [
        (cols_ref.at[:, pl.ds(0, EDGE)], cols_buf.at[:, pl.ds(0, EDGE)]),
        (cols_ref.at[:, pl.ds(width - EDGE, EDGE)], cols_buf.at[:, pl.ds(EDGE, EDGE)]),
        (sun_ref, pair_out.at[pl.ds(0, HALF)]),
        (shade_ref, pair_out.at[pl.ds(HALF, HALF)]),
        (frac_ref, frac_buf),
        (bias_sun_ref, bias_buf.at[pl.ds(0, 1)]),
        (bias_shade_ref, bias_buf.at[pl.ds(1, 1)]),
        (land_ref, land_buf),
        (mixing_ref, mixing_out),
        (cols_ref.at[:, pl.ds(EDGE, width - 2 * EDGE)], inner_out),
    ]
    copies = [pltpu.make_async_copy(a, b, sems.at[i]) for i, (a, b) in enumerate(moves)]
    for copy in copies:
        copy.start()
    for copy in copies[:-1]:
        copy.wait()
    bias = jnp.concatenate(
        [jnp.broadcast_to(bias_buf[i : i + 1, :], (HALF, HALF)).T for i in range(2)], axis=0
    )
    bias_out[...] = bias
    frac = frac_buf[...].astype(F32)
    frac_out[...] = frac
    count = land_buf[group_here()]
    column = lax.broadcasted_iota(jnp.int32, frac.shape, 0) * EDGE + lax.broadcasted_iota(jnp.int32, frac.shape, 1)
    land_out[...] = (column < count).astype(F32)
    land = jnp.concatenate([lanes(), lanes() + (width - EDGE)], axis=1) < count
    ends = jnp.concatenate([frac[:1], frac[frac.shape[0] - 1 :]], axis=1)
    raw = physics(
        cols_buf[...], ends, land, mixing_out[...], pair_out[...], jnp.concatenate([bias, bias], axis=1)
    )
    raw_first[...] = raw[:, :EDGE]
    raw_last[...] = raw[:, EDGE:]
    send_first[...] = raw[:, :EDGE].astype(BF16)
    send_last[...] = raw[:, EDGE:].astype(BF16)
    copies[-1].wait()


def inner_kernel(cols_ref, frac_ref, land_ref, mixing_ref, pair_ref, bias_ref, out_ref, buf, sems):
    bias = jnp.concatenate([bias_ref[...]] * (CHUNK // EDGE), axis=1)
    copies = []
    def spread(ref, row):
        return jnp.concatenate([ref[row + k : row + k + 1, :] for k in range(CHUNK // EDGE)], axis=1)

    for c in range(cols_ref.shape[1] // CHUNK):
        start = EDGE + c * CHUNK
        row = start // EDGE
        frac = spread(frac_ref, row)
        land = spread(land_ref, row) > 0.5
        raw = physics(cols_ref[:, c * CHUNK : (c + 1) * CHUNK], frac, land, mixing_ref[...], pair_ref[...], bias)
        buf[c] = raw.astype(BF16)
        copies.append(pltpu.make_async_copy(buf.at[c], out_ref.at[:, pl.ds(start, CHUNK)], sems.at[c]))
        copies[-1].start()
    for copy in copies:
        copy.wait()


def join_kernel(block, got_ref, own_ref, all_ref, out_ref, buf, sem):
    del all_ref
    buf[...] = (own_ref[...] + got_ref[...].astype(F32)).astype(BF16)
    copy = pltpu.make_async_copy(buf, out_ref.at[:, pl.ds(block * EDGE, EDGE)], sem)
    copy.start()
    copy.wait()


def off_chip(value):
    return pltpu.with_memory_space_constraint(value, pltpu.HBM)


def on_chip(value):
    return pltpu.with_memory_space_constraint(value, pltpu.VMEM)


HBM = pl.BlockSpec(memory_space=pltpu.HBM)
VMEM = pl.BlockSpec(memory_space=pltpu.VMEM)


def per_device(state, sun_frac, land_count, mixing, canopy_sun, canopy_shade, bias_sun, bias_shade):
    width = state.shape[2]
    cols = state.reshape(ROWS, width)
    groups = lax.axis_size(AXES)
    up = [(i, (i + 1) % groups) for i in range(groups)]
    down = [(b, a) for a, b in up]
    frac = sun_frac.reshape(width // EDGE, EDGE)
    chunks = (width - 2 * EDGE) // CHUNK

    send_first, send_last, raw_first, raw_last, mix, pair, bias, frac, land, inner = pl.pallas_call(
        edges_kernel,
        out_shape=(
            pltpu.VMEM((ROWS, EDGE), BF16),
            pltpu.VMEM((ROWS, EDGE), BF16),
            pltpu.VMEM((ROWS, EDGE), F32),
            pltpu.VMEM((ROWS, EDGE), F32),
            pltpu.VMEM((ROWS, ROWS), BF16),
            pltpu.VMEM((2 * HALF, HALF), BF16),
            pltpu.VMEM((2 * HALF, EDGE), F32),
            pltpu.VMEM((width // EDGE, EDGE), F32),
            pltpu.VMEM((width // EDGE, EDGE), F32),
            pltpu.VMEM((ROWS, width - 2 * EDGE), BF16),
        ),
        in_specs=[HBM] * 8,
        out_specs=[VMEM] * 10,
        scratch_shapes=[
            pltpu.VMEM((ROWS, 2 * EDGE), BF16),
            pltpu.VMEM((width // EDGE, EDGE), BF16),
            pltpu.VMEM((2, HALF), F32),
            pltpu.SMEM(land_count.shape, jnp.int32),
            pltpu.SemaphoreType.DMA((10,)),
        ],
        compiler_params=pltpu.CompilerParams(vmem_limit_bytes=VMEM_BYTES),
        name="edges",
    )(*map(off_chip, (land_count, cols, frac, mixing, canopy_sun, canopy_shade, bias_sun.reshape(1, HALF), bias_shade.reshape(1, HALF))))

    from_left = lax.ppermute(send_last, AXES, up)
    from_right = lax.ppermute(send_first, AXES, down)

    out = pl.pallas_call(
        inner_kernel,
        out_shape=jax.ShapeDtypeStruct((ROWS, width), BF16),
        in_specs=[VMEM] * 6,
        out_specs=HBM,
        scratch_shapes=[pltpu.VMEM((chunks, ROWS, CHUNK), BF16), pltpu.SemaphoreType.DMA((chunks,))],
        compiler_params=pltpu.CompilerParams(vmem_limit_bytes=VMEM_BYTES),
        name="inner",
    )(on_chip(inner), on_chip(frac), on_chip(land), on_chip(mix), on_chip(pair), on_chip(bias))

    def joined(out, got, own, block, name):
        def body(*refs):
            join_kernel(block, *refs)

        return pl.pallas_call(
            body,
            out_shape=jax.ShapeDtypeStruct((ROWS, width), BF16),
            in_specs=[VMEM, VMEM, HBM],
            out_specs=HBM,
            scratch_shapes=[pltpu.VMEM((ROWS, EDGE), BF16), pltpu.SemaphoreType.DMA],
            input_output_aliases={2: 0},
            compiler_params=pltpu.CompilerParams(vmem_limit_bytes=VMEM_BYTES),
            name=name,
        )(on_chip(got), on_chip(own), out)

    out = joined(out, from_left, raw_first, 0, "join_left")
    out = joined(out, from_right, raw_last, width // EDGE - 1, "join_right")
    return out.reshape(state.shape)


def solution(mesh):
    in_specs = (P(None, None, AXES), P(AXES), P(), P(), P(), P(), P(), P())
    out_specs = P(None, None, AXES)
    return jax.shard_map(
        per_device, mesh=mesh, in_specs=in_specs, out_specs=out_specs, check_vma=False
    )
```

```python
import jax
import jax.numpy as jnp
from jax import lax
from jax.experimental import pallas as pl
from jax.experimental.pallas import tpu as pltpu
from jax.sharding import PartitionSpec as P

FIELDS = 4
LEV = 128
CANLEV = 32
ITERS = 4
EDGE = 128
ROWS = FIELDS * LEV
HALF = FIELDS * CANLEV
CHUNK = 256
VMEM_BYTES = 16 * 2**20
AXES = ("seg", "sub")
F32 = jnp.float32
BF16 = jnp.bfloat16


def canopy_rows(values):
    return jnp.concatenate(
        [values[f * LEV + LEV - CANLEV : (f + 1) * LEV] for f in range(FIELDS)], axis=0
    )


def physics(cols, frac, land, mixing, pair, bias):
    raw = jnp.dot(mixing, cols, preferred_element_type=F32)
    rounded = canopy_rows(cols)
    low = rounded.astype(F32)
    of_sun = 0.5 * frac
    of_shade = 0.5 - of_sun
    current = low
    for step in range(ITERS):
        if step:
            rounded = current.astype(BF16)
        drive = jnp.tanh(jnp.dot(pair, rounded, preferred_element_type=F32) + bias)
        current = current + (of_sun * drive[:HALF] + of_shade * drive[HALF:])
    added = jnp.where(land, current - low, 0.0).astype(BF16).astype(F32)
    parts = []
    for f in range(FIELDS):
        top = f * LEV + LEV - CANLEV
        parts.append(raw[f * LEV : top])
        parts.append(raw[top : (f + 1) * LEV] + added[f * CANLEV : (f + 1) * CANLEV])
    return jnp.concatenate(parts, axis=0)


def group_here():
    return lax.axis_index("seg") * lax.axis_size("sub") + lax.axis_index("sub")


def relaxed(group):
    nsub = lax.axis_size("sub")
    return ((group // nsub) % 8 == 0) & (group >= nsub)


def lanes():
    return lax.broadcasted_iota(jnp.int32, (1, EDGE), 1)


def edges_kernel(
    land_ref, cols_ref, frac_ref, mixing_ref, sun_ref, shade_ref, bias_sun_ref, bias_shade_ref,
    send_first, send_last, send_mixed, raw_first, raw_last, mixing_out, pair_out, bias_out, frac_out, land_out, inner_out,
    cols_buf, frac_buf, bias_buf, land_buf, sems,
):
    width = cols_ref.shape[1]
    moves = [
        (cols_ref.at[:, pl.ds(0, EDGE)], cols_buf.at[:, pl.ds(0, EDGE)]),
        (cols_ref.at[:, pl.ds(width - EDGE, EDGE)], cols_buf.at[:, pl.ds(EDGE, EDGE)]),
        (sun_ref, pair_out.at[pl.ds(0, HALF)]),
        (shade_ref, pair_out.at[pl.ds(HALF, HALF)]),
        (frac_ref, frac_buf),
        (bias_sun_ref, bias_buf.at[pl.ds(0, 1)]),
        (bias_shade_ref, bias_buf.at[pl.ds(1, 1)]),
        (land_ref, land_buf),
        (mixing_ref, mixing_out),
        (cols_ref.at[:, pl.ds(EDGE, width - 2 * EDGE)], inner_out),
    ]
    copies = [pltpu.make_async_copy(a, b, sems.at[i]) for i, (a, b) in enumerate(moves)]
    for copy in copies:
        copy.start()
    for copy in copies[:-1]:
        copy.wait()
    bias = jnp.concatenate(
        [jnp.broadcast_to(bias_buf[i : i + 1, :], (HALF, HALF)).T for i in range(2)], axis=0
    )
    bias_out[...] = bias
    frac = frac_buf[...].astype(F32)
    frac_out[...] = frac
    count = land_buf[group_here()]
    column = lax.broadcasted_iota(jnp.int32, frac.shape, 0) * EDGE + lax.broadcasted_iota(jnp.int32, frac.shape, 1)
    land_out[...] = (column < count).astype(F32)
    land = jnp.concatenate([lanes(), lanes() + (width - EDGE)], axis=1) < count
    ends = jnp.concatenate([frac[:1], frac[frac.shape[0] - 1 :]], axis=1)
    raw = physics(
        cols_buf[...], ends, land, mixing_out[...], pair_out[...], jnp.concatenate([bias, bias], axis=1)
    )
    first, last = raw[:, :EDGE], raw[:, EDGE:]
    raw_first[...] = first
    raw_last[...] = last
    send_first[...] = first.astype(BF16)
    send_last[...] = last.astype(BF16)
    group = group_here()
    early_last = jnp.logical_and(group % 2 == 0, relaxed(group))

    @pl.when(early_last)
    def _():
        send_mixed[...] = last.astype(BF16)

    @pl.when(jnp.logical_not(early_last))
    def _():
        send_mixed[...] = first.astype(BF16)

    copies[-1].wait()


def inner_kernel(cols_ref, frac_ref, land_ref, mixing_ref, pair_ref, bias_ref, out_ref, buf, sems):
    bias = jnp.concatenate([bias_ref[...]] * (CHUNK // EDGE), axis=1)
    copies = []
    def spread(ref, row):
        return jnp.concatenate([ref[row + k : row + k + 1, :] for k in range(CHUNK // EDGE)], axis=1)

    for c in range(cols_ref.shape[1] // CHUNK):
        start = EDGE + c * CHUNK
        row = start // EDGE
        frac = spread(frac_ref, row)
        land = spread(land_ref, row) > 0.5
        raw = physics(cols_ref[:, c * CHUNK : (c + 1) * CHUNK], frac, land, mixing_ref[...], pair_ref[...], bias)
        buf[c] = raw.astype(BF16)
        copies.append(pltpu.make_async_copy(buf.at[c], out_ref.at[:, pl.ds(start, CHUNK)], sems.at[c]))
        copies[-1].start()
    for copy in copies:
        copy.wait()


def join_kernel(got_a, got_b, got_c, first_ref, last_ref, all_ref, out_ref, buf, sems):
    del all_ref
    group = group_here()
    groups = lax.axis_size(AXES)
    odd = group % 2 == 1
    left_in_b = jnp.logical_and(odd, relaxed(group))
    right_in_c = jnp.logical_and(odd, jnp.logical_or(relaxed(group), relaxed((group + 1) % groups)))
    copies = []
    for side, (own, usual, other, moved, start) in enumerate(
        (
            (first_ref, got_a, got_b, left_in_b, 0),
            (last_ref, got_b, got_c, right_in_c, out_ref.shape[1] - EDGE),
        )
    ):
        for flag, got in ((jnp.logical_not(moved), usual), (moved, other)):

            @pl.when(flag)
            def _(side=side, own=own, got=got):
                buf[side] = (own[...] + got[...].astype(F32)).astype(BF16)

        copies.append(pltpu.make_async_copy(buf.at[side], out_ref.at[:, pl.ds(start, EDGE)], sems.at[side]))
        copies[-1].start()
    for copy in copies:
        copy.wait()


def off_chip(value):
    return pltpu.with_memory_space_constraint(value, pltpu.HBM)


def on_chip(value):
    return pltpu.with_memory_space_constraint(value, pltpu.VMEM)


HBM = pl.BlockSpec(memory_space=pltpu.HBM)
VMEM = pl.BlockSpec(memory_space=pltpu.VMEM)


def per_device(state, sun_frac, land_count, mixing, canopy_sun, canopy_shade, bias_sun, bias_shade):
    width = state.shape[2]
    cols = state.reshape(ROWS, width)
    groups = lax.axis_size(AXES)
    pairs = {"a": [], "b": [], "c": []}
    for i in range(groups):
        nxt = (i + 1) % groups
        if i % 2:
            pairs["a"].append((i, nxt))
            pairs["c" if relaxed(i) | relaxed(nxt) else "b"].append((nxt, i))
        else:
            pairs["b" if relaxed(i) else "a"].append((i, nxt))
            pairs["b"].append((nxt, i))
    frac = sun_frac.reshape(width // EDGE, EDGE)
    chunks = (width - 2 * EDGE) // CHUNK

    send_first, send_last, send_mixed, raw_first, raw_last, mix, pair, bias, frac, land, inner = pl.pallas_call(
        edges_kernel,
        out_shape=(
            pltpu.VMEM((ROWS, EDGE), BF16),
            pltpu.VMEM((ROWS, EDGE), BF16),
            pltpu.VMEM((ROWS, EDGE), BF16),
            pltpu.VMEM((ROWS, EDGE), F32),
            pltpu.VMEM((ROWS, EDGE), F32),
            pltpu.VMEM((ROWS, ROWS), BF16),
            pltpu.VMEM((2 * HALF, HALF), BF16),
            pltpu.VMEM((2 * HALF, EDGE), F32),
            pltpu.VMEM((width // EDGE, EDGE), F32),
            pltpu.VMEM((width // EDGE, EDGE), F32),
            pltpu.VMEM((ROWS, width - 2 * EDGE), BF16),
        ),
        in_specs=[HBM] * 8,
        out_specs=[VMEM] * 11,
        scratch_shapes=[
            pltpu.VMEM((ROWS, 2 * EDGE), BF16),
            pltpu.VMEM((width // EDGE, EDGE), BF16),
            pltpu.VMEM((2, HALF), F32),
            pltpu.SMEM(land_count.shape, jnp.int32),
            pltpu.SemaphoreType.DMA((10,)),
        ],
        compiler_params=pltpu.CompilerParams(vmem_limit_bytes=VMEM_BYTES),
        name="edges",
    )(*map(off_chip, (land_count, cols, frac, mixing, canopy_sun, canopy_shade, bias_sun.reshape(1, HALF), bias_shade.reshape(1, HALF))))

    got_a = lax.ppermute(send_last, AXES, pairs["a"])
    got_b = lax.ppermute(send_mixed, AXES, pairs["b"])
    got_c = lax.ppermute(send_first, AXES, pairs["c"])

    out = pl.pallas_call(
        inner_kernel,
        out_shape=jax.ShapeDtypeStruct((ROWS, width), BF16),
        in_specs=[VMEM] * 6,
        out_specs=HBM,
        scratch_shapes=[pltpu.VMEM((chunks, ROWS, CHUNK), BF16), pltpu.SemaphoreType.DMA((chunks,))],
        compiler_params=pltpu.CompilerParams(vmem_limit_bytes=VMEM_BYTES),
        name="inner",
    )(on_chip(inner), on_chip(frac), on_chip(land), on_chip(mix), on_chip(pair), on_chip(bias))

    out = pl.pallas_call(
        join_kernel,
        out_shape=jax.ShapeDtypeStruct((ROWS, width), BF16),
        in_specs=[*[VMEM] * 5, HBM],
        out_specs=HBM,
        scratch_shapes=[pltpu.VMEM((2, ROWS, EDGE), BF16), pltpu.SemaphoreType.DMA((2,))],
        input_output_aliases={5: 0},
        compiler_params=pltpu.CompilerParams(vmem_limit_bytes=VMEM_BYTES),
        name="join",
    )(*map(on_chip, (got_a, got_b, got_c, raw_first, raw_last)), out)
    return out.reshape(state.shape)


def solution(mesh):
    in_specs = (P(None, None, AXES), P(AXES), P(), P(), P(), P(), P(), P())
    out_specs = P(None, None, AXES)
    return jax.shard_map(
        per_device, mesh=mesh, in_specs=in_specs, out_specs=out_specs, check_vma=False
    )
```

```python
import jax
import jax.numpy as jnp
from jax import lax
from jax.experimental import pallas as pl
from jax.experimental.pallas import tpu as pltpu
from jax.sharding import PartitionSpec as P

FIELDS = 4
LEV = 128
CANLEV = 32
ITERS = 4
EDGE = 128
ROWS = FIELDS * LEV
HALF = FIELDS * CANLEV
CHUNK = 256
VMEM_BYTES = 16 * 2**20
AXES = ("seg", "sub")
F32 = jnp.float32
BF16 = jnp.bfloat16


def canopy_rows(values):
    return jnp.concatenate(
        [values[f * LEV + LEV - CANLEV : (f + 1) * LEV] for f in range(FIELDS)], axis=0
    )


def physics(cols, frac, land, mixing, pair, bias):
    raw = jnp.dot(mixing, cols, preferred_element_type=F32)
    rounded = canopy_rows(cols)
    low = rounded.astype(F32)
    of_sun = 0.5 * frac
    of_shade = 0.5 - of_sun
    current = low
    for step in range(ITERS):
        if step:
            rounded = current.astype(BF16)
        drive = jnp.tanh(jnp.dot(pair, rounded, preferred_element_type=F32) + bias)
        current = current + (of_sun * drive[:HALF] + of_shade * drive[HALF:])
    added = jnp.where(land, current - low, 0.0).astype(BF16).astype(F32)
    parts = []
    for f in range(FIELDS):
        top = f * LEV + LEV - CANLEV
        parts.append(raw[f * LEV : top])
        parts.append(raw[top : (f + 1) * LEV] + added[f * CANLEV : (f + 1) * CANLEV])
    return jnp.concatenate(parts, axis=0)


def group_here():
    return lax.axis_index("seg") * lax.axis_size("sub") + lax.axis_index("sub")


def relaxed(group):
    nsub = lax.axis_size("sub")
    return ((group // nsub) % 8 == 0) & (group >= nsub)


def patient(group):
    return (group // (2 * lax.axis_size("sub"))) % 4 >= 2


def lanes():
    return lax.broadcasted_iota(jnp.int32, (1, EDGE), 1)


def edges_kernel(
    land_ref, cols_ref, frac_ref, mixing_ref, sun_ref, shade_ref, bias_sun_ref, bias_shade_ref,
    send_first, send_last, send_mixed, raw_first, raw_last, mixing_out, pair_out, bias_out, frac_out, land_out, inner_out,
    cols_buf, frac_buf, bias_buf, land_buf, sems,
):
    width = cols_ref.shape[1]
    moves = [
        (cols_ref.at[:, pl.ds(0, EDGE)], cols_buf.at[:, pl.ds(0, EDGE)]),
        (cols_ref.at[:, pl.ds(width - EDGE, EDGE)], cols_buf.at[:, pl.ds(EDGE, EDGE)]),
        (sun_ref, pair_out.at[pl.ds(0, HALF)]),
        (shade_ref, pair_out.at[pl.ds(HALF, HALF)]),
        (frac_ref, frac_buf),
        (bias_sun_ref, bias_buf.at[pl.ds(0, 1)]),
        (bias_shade_ref, bias_buf.at[pl.ds(1, 1)]),
        (land_ref, land_buf),
        (mixing_ref, mixing_out),
        (cols_ref.at[:, pl.ds(EDGE, width - 2 * EDGE)], inner_out),
    ]
    copies = [pltpu.make_async_copy(a, b, sems.at[i]) for i, (a, b) in enumerate(moves)]
    for copy in copies:
        copy.start()
    for copy in copies[:-1]:
        copy.wait()
    bias = jnp.concatenate(
        [jnp.broadcast_to(bias_buf[i : i + 1, :], (HALF, HALF)).T for i in range(2)], axis=0
    )
    bias_out[...] = bias
    frac = frac_buf[...].astype(F32)
    frac_out[...] = frac
    count = land_buf[group_here()]
    column = lax.broadcasted_iota(jnp.int32, frac.shape, 0) * EDGE + lax.broadcasted_iota(jnp.int32, frac.shape, 1)
    land_out[...] = (column < count).astype(F32)
    land = jnp.concatenate([lanes(), lanes() + (width - EDGE)], axis=1) < count
    ends = jnp.concatenate([frac[:1], frac[frac.shape[0] - 1 :]], axis=1)
    raw = physics(
        cols_buf[...], ends, land, mixing_out[...], pair_out[...], jnp.concatenate([bias, bias], axis=1)
    )
    first, last = raw[:, :EDGE], raw[:, EDGE:]
    raw_first[...] = first
    raw_last[...] = last
    send_first[...] = first.astype(BF16)
    send_last[...] = last.astype(BF16)
    group = group_here()
    early_last = jnp.logical_and(group % 2 == 0, relaxed(group))

    @pl.when(early_last)
    def _():
        send_mixed[...] = last.astype(BF16)

    @pl.when(jnp.logical_not(early_last))
    def _():
        send_mixed[...] = first.astype(BF16)

    copies[-1].wait()


def inner_kernel(cols_ref, frac_ref, land_ref, mixing_ref, pair_ref, bias_ref, out_ref, buf, sems):
    bias = jnp.concatenate([bias_ref[...]] * (CHUNK // EDGE), axis=1)
    copies = []
    def spread(ref, row):
        return jnp.concatenate([ref[row + k : row + k + 1, :] for k in range(CHUNK // EDGE)], axis=1)

    for c in range(cols_ref.shape[1] // CHUNK):
        start = EDGE + c * CHUNK
        row = start // EDGE
        frac = spread(frac_ref, row)
        land = spread(land_ref, row) > 0.5
        raw = physics(cols_ref[:, c * CHUNK : (c + 1) * CHUNK], frac, land, mixing_ref[...], pair_ref[...], bias)
        buf[c] = raw.astype(BF16)
        copies.append(pltpu.make_async_copy(buf.at[c], out_ref.at[:, pl.ds(start, CHUNK)], sems.at[c]))
        copies[-1].start()
    for copy in copies:
        copy.wait()


def join_kernel(got_a, got_b, got_c, first_ref, last_ref, all_ref, out_ref, buf, sems):
    del all_ref
    group = group_here()
    groups = lax.axis_size(AXES)
    odd = group % 2 == 1
    left_in_b = jnp.logical_and(odd, relaxed(group))
    right_in_c = jnp.logical_and(odd, jnp.logical_or(relaxed(group), relaxed((group + 1) % groups)))
    right_in_c = jnp.logical_or(right_in_c, patient(group))
    copies = []
    for side, (own, usual, other, moved, start) in enumerate(
        (
            (first_ref, got_a, got_b, left_in_b, 0),
            (last_ref, got_b, got_c, right_in_c, out_ref.shape[1] - EDGE),
        )
    ):
        for flag, got in ((jnp.logical_not(moved), usual), (moved, other)):

            @pl.when(flag)
            def _(side=side, own=own, got=got):
                buf[side] = (own[...] + got[...].astype(F32)).astype(BF16)

        copies.append(pltpu.make_async_copy(buf.at[side], out_ref.at[:, pl.ds(start, EDGE)], sems.at[side]))
        copies[-1].start()
    for copy in copies:
        copy.wait()


def off_chip(value):
    return pltpu.with_memory_space_constraint(value, pltpu.HBM)


def on_chip(value):
    return pltpu.with_memory_space_constraint(value, pltpu.VMEM)


HBM = pl.BlockSpec(memory_space=pltpu.HBM)
VMEM = pl.BlockSpec(memory_space=pltpu.VMEM)


def per_device(state, sun_frac, land_count, mixing, canopy_sun, canopy_shade, bias_sun, bias_shade):
    width = state.shape[2]
    cols = state.reshape(ROWS, width)
    groups = lax.axis_size(AXES)
    pairs = {"a": [], "b": [], "c": []}
    for i in range(groups):
        nxt = (i + 1) % groups
        if i % 2:
            pairs["a"].append((i, nxt))
            pairs["c" if relaxed(i) | relaxed(nxt) | patient(i) else "b"].append((nxt, i))
        else:
            pairs["b" if relaxed(i) else "a"].append((i, nxt))
            pairs["c" if patient(i) else "b"].append((nxt, i))
    frac = sun_frac.reshape(width // EDGE, EDGE)
    chunks = (width - 2 * EDGE) // CHUNK

    send_first, send_last, send_mixed, raw_first, raw_last, mix, pair, bias, frac, land, inner = pl.pallas_call(
        edges_kernel,
        out_shape=(
            pltpu.VMEM((ROWS, EDGE), BF16),
            pltpu.VMEM((ROWS, EDGE), BF16),
            pltpu.VMEM((ROWS, EDGE), BF16),
            pltpu.VMEM((ROWS, EDGE), F32),
            pltpu.VMEM((ROWS, EDGE), F32),
            pltpu.VMEM((ROWS, ROWS), BF16),
            pltpu.VMEM((2 * HALF, HALF), BF16),
            pltpu.VMEM((2 * HALF, EDGE), F32),
            pltpu.VMEM((width // EDGE, EDGE), F32),
            pltpu.VMEM((width // EDGE, EDGE), F32),
            pltpu.VMEM((ROWS, width - 2 * EDGE), BF16),
        ),
        in_specs=[HBM] * 8,
        out_specs=[VMEM] * 11,
        scratch_shapes=[
            pltpu.VMEM((ROWS, 2 * EDGE), BF16),
            pltpu.VMEM((width // EDGE, EDGE), BF16),
            pltpu.VMEM((2, HALF), F32),
            pltpu.SMEM(land_count.shape, jnp.int32),
            pltpu.SemaphoreType.DMA((10,)),
        ],
        compiler_params=pltpu.CompilerParams(vmem_limit_bytes=VMEM_BYTES),
        name="edges",
    )(*map(off_chip, (land_count, cols, frac, mixing, canopy_sun, canopy_shade, bias_sun.reshape(1, HALF), bias_shade.reshape(1, HALF))))

    got_a = lax.ppermute(send_last, AXES, pairs["a"])
    got_b = lax.ppermute(send_mixed, AXES, pairs["b"])
    got_c = lax.ppermute(send_first, AXES, pairs["c"])

    out = pl.pallas_call(
        inner_kernel,
        out_shape=jax.ShapeDtypeStruct((ROWS, width), BF16),
        in_specs=[VMEM] * 6,
        out_specs=HBM,
        scratch_shapes=[pltpu.VMEM((chunks, ROWS, CHUNK), BF16), pltpu.SemaphoreType.DMA((chunks,))],
        compiler_params=pltpu.CompilerParams(vmem_limit_bytes=VMEM_BYTES),
        name="inner",
    )(on_chip(inner), on_chip(frac), on_chip(land), on_chip(mix), on_chip(pair), on_chip(bias))

    out = pl.pallas_call(
        join_kernel,
        out_shape=jax.ShapeDtypeStruct((ROWS, width), BF16),
        in_specs=[*[VMEM] * 5, HBM],
        out_specs=HBM,
        scratch_shapes=[pltpu.VMEM((2, ROWS, EDGE), BF16), pltpu.SemaphoreType.DMA((2,))],
        input_output_aliases={5: 0},
        compiler_params=pltpu.CompilerParams(vmem_limit_bytes=VMEM_BYTES),
        name="join",
    )(*map(on_chip, (got_a, got_b, got_c, raw_first, raw_last)), out)
    return out.reshape(state.shape)


def solution(mesh):
    in_specs = (P(None, None, AXES), P(AXES), P(), P(), P(), P(), P(), P())
    out_specs = P(None, None, AXES)
    return jax.shard_map(
        per_device, mesh=mesh, in_specs=in_specs, out_specs=out_specs, check_vma=False
    )
```

```python
import jax
import jax.numpy as jnp
from jax import lax
from jax.experimental import pallas as pl
from jax.experimental.pallas import tpu as pltpu
from jax.sharding import PartitionSpec as P

FIELDS = 4
LEV = 128
CANLEV = 32
ITERS = 4
EDGE = 128
ROWS = FIELDS * LEV
HALF = FIELDS * CANLEV
CHUNK = 256
VMEM_BYTES = 16 * 2**20
AXES = ("seg", "sub")
F32 = jnp.float32
BF16 = jnp.bfloat16


def canopy_rows(values):
    return jnp.concatenate(
        [values[f * LEV + LEV - CANLEV : (f + 1) * LEV] for f in range(FIELDS)], axis=0
    )


def physics(cols, frac, land, mixing, pair, bias):
    raw = jnp.dot(mixing, cols, preferred_element_type=F32)
    rounded = canopy_rows(cols)
    low = rounded.astype(F32)
    of_sun = 0.5 * frac
    of_shade = 0.5 - of_sun
    current = low
    for step in range(ITERS):
        if step:
            rounded = current.astype(BF16)
        drive = jnp.tanh(jnp.dot(pair, rounded, preferred_element_type=F32) + bias)
        current = current + (of_sun * drive[:HALF] + of_shade * drive[HALF:])
    added = jnp.where(land, current - low, 0.0).astype(BF16).astype(F32)
    parts = []
    for f in range(FIELDS):
        top = f * LEV + LEV - CANLEV
        parts.append(raw[f * LEV : top])
        parts.append(raw[top : (f + 1) * LEV] + added[f * CANLEV : (f + 1) * CANLEV])
    return jnp.concatenate(parts, axis=0)


def group_here():
    return lax.axis_index("seg") * lax.axis_size("sub") + lax.axis_index("sub")


def relaxed(group):
    nsub = lax.axis_size("sub")
    return ((group // nsub) % 8 == 0) & (group >= nsub)


def patient(group):
    return (group // (2 * lax.axis_size("sub"))) % 4 == 3


def lanes():
    return lax.broadcasted_iota(jnp.int32, (1, EDGE), 1)


def edges_kernel(
    land_ref, cols_ref, frac_ref, mixing_ref, sun_ref, shade_ref, bias_sun_ref, bias_shade_ref,
    send_first, send_last, send_mixed, raw_first, raw_last, mixing_out, pair_out, bias_out, frac_out, land_out, inner_out,
    cols_buf, frac_buf, bias_buf, land_buf, sems,
):
    width = cols_ref.shape[1]
    moves = [
        (cols_ref.at[:, pl.ds(0, EDGE)], cols_buf.at[:, pl.ds(0, EDGE)]),
        (cols_ref.at[:, pl.ds(width - EDGE, EDGE)], cols_buf.at[:, pl.ds(EDGE, EDGE)]),
        (sun_ref, pair_out.at[pl.ds(0, HALF)]),
        (shade_ref, pair_out.at[pl.ds(HALF, HALF)]),
        (frac_ref, frac_buf),
        (bias_sun_ref, bias_buf.at[pl.ds(0, 1)]),
        (bias_shade_ref, bias_buf.at[pl.ds(1, 1)]),
        (land_ref, land_buf),
        (mixing_ref, mixing_out),
        (cols_ref.at[:, pl.ds(EDGE, width - 2 * EDGE)], inner_out),
    ]
    copies = [pltpu.make_async_copy(a, b, sems.at[i]) for i, (a, b) in enumerate(moves)]
    for copy in copies:
        copy.start()
    for copy in copies[:-1]:
        copy.wait()
    bias = jnp.concatenate(
        [jnp.broadcast_to(bias_buf[i : i + 1, :], (HALF, HALF)).T for i in range(2)], axis=0
    )
    bias_out[...] = bias
    frac = frac_buf[...].astype(F32)
    frac_out[...] = frac
    count = land_buf[group_here()]
    column = lax.broadcasted_iota(jnp.int32, frac.shape, 0) * EDGE + lax.broadcasted_iota(jnp.int32, frac.shape, 1)
    land_out[...] = (column < count).astype(F32)
    land = jnp.concatenate([lanes(), lanes() + (width - EDGE)], axis=1) < count
    ends = jnp.concatenate([frac[:1], frac[frac.shape[0] - 1 :]], axis=1)
    raw = physics(
        cols_buf[...], ends, land, mixing_out[...], pair_out[...], jnp.concatenate([bias, bias], axis=1)
    )
    first, last = raw[:, :EDGE], raw[:, EDGE:]
    raw_first[...] = first
    raw_last[...] = last
    send_first[...] = first.astype(BF16)
    send_last[...] = last.astype(BF16)
    group = group_here()
    early_last = jnp.logical_and(group % 2 == 0, relaxed(group))

    @pl.when(early_last)
    def _():
        send_mixed[...] = last.astype(BF16)

    @pl.when(jnp.logical_not(early_last))
    def _():
        send_mixed[...] = first.astype(BF16)

    copies[-1].wait()


def inner_kernel(cols_ref, frac_ref, land_ref, mixing_ref, pair_ref, bias_ref, out_ref, buf, sems):
    bias = jnp.concatenate([bias_ref[...]] * (CHUNK // EDGE), axis=1)
    copies = []
    def spread(ref, row):
        return jnp.concatenate([ref[row + k : row + k + 1, :] for k in range(CHUNK // EDGE)], axis=1)

    for c in range(cols_ref.shape[1] // CHUNK):
        start = EDGE + c * CHUNK
        row = start // EDGE
        frac = spread(frac_ref, row)
        land = spread(land_ref, row) > 0.5
        raw = physics(cols_ref[:, c * CHUNK : (c + 1) * CHUNK], frac, land, mixing_ref[...], pair_ref[...], bias)
        buf[c] = raw.astype(BF16)
        copies.append(pltpu.make_async_copy(buf.at[c], out_ref.at[:, pl.ds(start, CHUNK)], sems.at[c]))
        copies[-1].start()
    for copy in copies:
        copy.wait()


def join_kernel(got_a, got_b, got_c, first_ref, last_ref, all_ref, out_ref, buf, sems):
    del all_ref
    group = group_here()
    groups = lax.axis_size(AXES)
    odd = group % 2 == 1
    left_in_b = jnp.logical_and(odd, relaxed(group))
    right_in_c = jnp.logical_and(odd, jnp.logical_or(relaxed(group), relaxed((group + 1) % groups)))
    right_in_c = jnp.logical_or(right_in_c, patient(group))
    copies = []
    for side, (own, usual, other, moved, start) in enumerate(
        (
            (first_ref, got_a, got_b, left_in_b, 0),
            (last_ref, got_b, got_c, right_in_c, out_ref.shape[1] - EDGE),
        )
    ):
        for flag, got in ((jnp.logical_not(moved), usual), (moved, other)):

            @pl.when(flag)
            def _(side=side, own=own, got=got):
                buf[side] = (own[...] + got[...].astype(F32)).astype(BF16)

        copies.append(pltpu.make_async_copy(buf.at[side], out_ref.at[:, pl.ds(start, EDGE)], sems.at[side]))
        copies[-1].start()
    for copy in copies:
        copy.wait()


def off_chip(value):
    return pltpu.with_memory_space_constraint(value, pltpu.HBM)


def on_chip(value):
    return pltpu.with_memory_space_constraint(value, pltpu.VMEM)


HBM = pl.BlockSpec(memory_space=pltpu.HBM)
VMEM = pl.BlockSpec(memory_space=pltpu.VMEM)


def per_device(state, sun_frac, land_count, mixing, canopy_sun, canopy_shade, bias_sun, bias_shade):
    width = state.shape[2]
    cols = state.reshape(ROWS, width)
    groups = lax.axis_size(AXES)
    pairs = {"a": [], "b": [], "c": []}
    for i in range(groups):
        nxt = (i + 1) % groups
        if i % 2:
            pairs["a"].append((i, nxt))
            pairs["c" if relaxed(i) | relaxed(nxt) | patient(i) else "b"].append((nxt, i))
        else:
            pairs["b" if relaxed(i) else "a"].append((i, nxt))
            pairs["c" if patient(i) else "b"].append((nxt, i))
    frac = sun_frac.reshape(width // EDGE, EDGE)
    chunks = (width - 2 * EDGE) // CHUNK

    send_first, send_last, send_mixed, raw_first, raw_last, mix, pair, bias, frac, land, inner = pl.pallas_call(
        edges_kernel,
        out_shape=(
            pltpu.VMEM((ROWS, EDGE), BF16),
            pltpu.VMEM((ROWS, EDGE), BF16),
            pltpu.VMEM((ROWS, EDGE), BF16),
            pltpu.VMEM((ROWS, EDGE), F32),
            pltpu.VMEM((ROWS, EDGE), F32),
            pltpu.VMEM((ROWS, ROWS), BF16),
            pltpu.VMEM((2 * HALF, HALF), BF16),
            pltpu.VMEM((2 * HALF, EDGE), F32),
            pltpu.VMEM((width // EDGE, EDGE), F32),
            pltpu.VMEM((width // EDGE, EDGE), F32),
            pltpu.VMEM((ROWS, width - 2 * EDGE), BF16),
        ),
        in_specs=[HBM] * 8,
        out_specs=[VMEM] * 11,
        scratch_shapes=[
            pltpu.VMEM((ROWS, 2 * EDGE), BF16),
            pltpu.VMEM((width // EDGE, EDGE), BF16),
            pltpu.VMEM((2, HALF), F32),
            pltpu.SMEM(land_count.shape, jnp.int32),
            pltpu.SemaphoreType.DMA((10,)),
        ],
        compiler_params=pltpu.CompilerParams(vmem_limit_bytes=VMEM_BYTES),
        name="edges",
    )(*map(off_chip, (land_count, cols, frac, mixing, canopy_sun, canopy_shade, bias_sun.reshape(1, HALF), bias_shade.reshape(1, HALF))))

    got_a = lax.ppermute(send_last, AXES, pairs["a"])
    got_b = lax.ppermute(send_mixed, AXES, pairs["b"])
    got_c = lax.ppermute(send_first, AXES, pairs["c"])

    out = pl.pallas_call(
        inner_kernel,
        out_shape=jax.ShapeDtypeStruct((ROWS, width), BF16),
        in_specs=[VMEM] * 6,
        out_specs=HBM,
        scratch_shapes=[pltpu.VMEM((chunks, ROWS, CHUNK), BF16), pltpu.SemaphoreType.DMA((chunks,))],
        compiler_params=pltpu.CompilerParams(vmem_limit_bytes=VMEM_BYTES),
        name="inner",
    )(on_chip(inner), on_chip(frac), on_chip(land), on_chip(mix), on_chip(pair), on_chip(bias))

    out = pl.pallas_call(
        join_kernel,
        out_shape=jax.ShapeDtypeStruct((ROWS, width), BF16),
        in_specs=[*[VMEM] * 5, HBM],
        out_specs=HBM,
        scratch_shapes=[pltpu.VMEM((2, ROWS, EDGE), BF16), pltpu.SemaphoreType.DMA((2,))],
        input_output_aliases={5: 0},
        compiler_params=pltpu.CompilerParams(vmem_limit_bytes=VMEM_BYTES),
        name="join",
    )(*map(on_chip, (got_a, got_b, got_c, raw_first, raw_last)), out)
    return out.reshape(state.shape)


def solution(mesh):
    in_specs = (P(None, None, AXES), P(AXES), P(), P(), P(), P(), P(), P())
    out_specs = P(None, None, AXES)
    return jax.shard_map(
        per_device, mesh=mesh, in_specs=in_specs, out_specs=out_specs, check_vma=False
    )
```
